32 devices in a mesh: pipe: 4 (over y, x), ctx: 8 (over z, core).
Axes of the slice: x: 2, y: 2, z: 4, core: 2. Of those that a mesh axis runs over, the one named last changes fastest.
Arguments:
- queries: bfloat16 [4, 1, 1024, 3072], P('pipe', None, 'ctx'), may hold values from -24 to 24
- projected_key_value: bfloat16 [4, 1, 1024, 1024], P('pipe', None, 'ctx'), may hold values from -24 to 24
- layout: int32 [1, 1, 16], replicated, may hold values from 0 to 15, each once within a row
Outputs:
- arrived: bfloat16 [4, 1, 1024, 3072], P('pipe', None, 'ctx')
The draws below stay inside these ranges and needn't reach their ends.
Inputs may be any that keep to these rules, and one draw needn't show every extreme that they name: Every row of layout names each of the 16 token blocks once.
All inputs are finite; a program needn't handle non-finite values.
Results may differ from the reference program's by a relative error of at most 0.0055.
Values may be sent and summed in bfloat16 or wider, within the bound.
A program may use at most 64 MiB of HBM per device.

```python
import math
import jax
import jax.numpy as jnp
from jax import lax

HQ = 24
KEY_VALUE_HEADS = 4
HEAD_SIZE = 128
QUERY_PER_KV = 6
TOK_DEV = 128
MICRO_BATCHES = 1
SEQ_DEVS = 8
MICRO_SEQUENCES = 1
BLOCKS = 16
RELAY_SECTIONS = 4
MICRO_TOKENS = 1024


def joint_draw(key):
    query_layout_shape = (RELAY_SECTIONS, MICRO_BATCHES, MICRO_TOKENS, KEY_VALUE_HEADS, QUERY_PER_KV, HEAD_SIZE)
    key_layout_shape = (RELAY_SECTIONS, MICRO_BATCHES, MICRO_TOKENS, KEY_VALUE_HEADS, HEAD_SIZE)
    base_q = jnp.clip(jax.random.normal(jax.random.fold_in(key, 11), query_layout_shape, jnp.float32), -4.0, 4.0)
    base_k = jnp.clip(jax.random.normal(jax.random.fold_in(key, 12), key_layout_shape, jnp.float32), -4.0, 4.0)
    value_portion = jnp.clip(jax.random.normal(jax.random.fold_in(key, 13), key_layout_shape, jnp.float32), -4.0, 4.0)
    query_part = base_q
    key_portion = base_k
    query_flat = query_part.reshape(RELAY_SECTIONS, MICRO_BATCHES, MICRO_TOKENS, HQ * HEAD_SIZE)
    key_value_flat = jnp.concatenate([key_portion.reshape(RELAY_SECTIONS, MICRO_BATCHES, MICRO_TOKENS, KEY_VALUE_HEADS * HEAD_SIZE), value_portion.reshape(RELAY_SECTIONS, MICRO_BATCHES, MICRO_TOKENS, KEY_VALUE_HEADS * HEAD_SIZE)], axis=-1)
    return (query_flat, key_value_flat)


def draw_queries(key, part):
    return joint_draw(key)[0].astype(jnp.bfloat16)


def draw_projected_key_value(key, part):
    return joint_draw(key)[1].astype(jnp.bfloat16)


def setup_inputs(seed: int = 0) -> dict:
    splits = jax.random.split(jax.random.key(seed), 4)
    return {
        "queries": draw_queries(jax.random.fold_in(splits[3], 71), 0),
        "projected_key_value": draw_projected_key_value(jax.random.fold_in(splits[3], 71), 0),
        "layout": jax.vmap(lambda own: jax.random.permutation(own, BLOCKS))(jax.random.split(splits[2], MICRO_BATCHES * MICRO_SEQUENCES)).reshape((MICRO_BATCHES, MICRO_SEQUENCES, BLOCKS)).astype(jnp.int32),
    }


def reference(queries, projected_key_value, layout):
    block_rows = TOK_DEV // 2
    portion_length = SEQ_DEVS * TOK_DEV
    score_scale = 1.0 / math.sqrt(HEAD_SIZE)
    row_iota = jnp.arange(portion_length, dtype=jnp.int32)
    slot_index = row_iota // block_rows
    offsets = row_iota % block_rows
    positions = layout[:, :, slot_index] * block_rows + offsets[None, None, :]
    reshaped_query = queries.reshape(RELAY_SECTIONS, MICRO_BATCHES, MICRO_SEQUENCES, portion_length, KEY_VALUE_HEADS, QUERY_PER_KV, HEAD_SIZE)
    reshaped_key_value = projected_key_value.reshape(RELAY_SECTIONS, MICRO_BATCHES, MICRO_SEQUENCES, portion_length, 2, KEY_VALUE_HEADS, HEAD_SIZE)

    def single(flat_index):
        section = flat_index // (MICRO_BATCHES * MICRO_SEQUENCES)
        micro = flat_index // MICRO_SEQUENCES % MICRO_BATCHES
        sequence = flat_index % MICRO_SEQUENCES
        query_tile_rows = reshaped_query[section, micro, sequence].astype(jnp.float32)
        key_tile_rows = reshaped_key_value[section, micro, sequence, :, 0].astype(jnp.float32)
        value_tile_rows = reshaped_key_value[section, micro, sequence, :, 1].astype(jnp.float32)
        seq_pos = positions[micro, sequence]
        scores = jnp.einsum('ihgd,jhd->hgij', query_tile_rows, key_tile_rows) * score_scale
        allowed = seq_pos[None, :] <= seq_pos[:, None]
        scores = jnp.where(allowed[None, None], scores, -1e+30)
        row_max = lax.optimization_barrier(jnp.max(scores, axis=3))
        expo = jnp.exp(scores - row_max[..., None])
        totals = lax.optimization_barrier(jnp.sum(expo, axis=3))
        weights = expo.astype(jnp.bfloat16).astype(jnp.float32)
        numer = jnp.einsum('hgij,jhd->ihgd', weights, value_tile_rows)
        result = numer / jnp.transpose(totals, (2, 0, 1))[..., None]
        return result.astype(jnp.bfloat16).reshape(portion_length, HQ * HEAD_SIZE)
    outputs = lax.map(single, jnp.arange(RELAY_SECTIONS * MICRO_BATCHES * MICRO_SEQUENCES, dtype=jnp.int32))
    attended = outputs.reshape(RELAY_SECTIONS, MICRO_BATCHES, MICRO_TOKENS, HQ * HEAD_SIZE)
    return jnp.roll(attended, 1, axis=0)
```

```python
import functools
import math

import jax
import jax.numpy as jnp
from jax import lax
from jax.experimental import pallas as pl
from jax.experimental.pallas import tpu as pltpu
from jax.sharding import PartitionSpec as P

HEAD_SIZE = 128
MESH = pl.DeviceIdType.MESH
STACK = 2
LEAD = 2


def kernel(
    n, sections, key_heads, per_kv,
    layout_ref, q_hbm, kv_hbm, out_ref,
    q_buf, kv_all, att, bias, local_sem, send_sem, recv_sem, out_send, out_recv,
):
    rows = q_buf.shape[0]
    block = rows // 2
    chips = n // 2
    section = lax.axis_index("pipe")
    me = lax.axis_index("ctx")
    place = me // 2
    core = me % 2
    width = key_heads * HEAD_SIZE

    def at_ctx(index):
        return {"pipe": section, "ctx": index}

    after = (section + 1) % sections
    before = (section + sections - 1) % sections
    has_right = place < chips - 1
    has_left = place > 0
    sibling = 2 * place + 1 - core

    def own_copy(head, half):
        return pltpu.make_async_copy(
            kv_hbm.at[:, pl.ds(half * width + head * HEAD_SIZE, HEAD_SIZE)],
            kv_all.at[head, me, :, pl.ds(half * HEAD_SIZE, HEAD_SIZE)],
            local_sem.at[2 * head + half],
        )

    q_copy = pltpu.make_async_copy(q_hbm, q_buf, local_sem.at[2 * key_heads])
    for head in range(key_heads):
        own_copy(head, 0).start()
        own_copy(head, 1).start()
    q_copy.start()

    barrier = pltpu.get_barrier_semaphore()
    pl.semaphore_signal(barrier, inc=1, device_id=at_ctx(sibling), device_id_type=MESH)
    for other in (after, before):
        pl.semaphore_signal(
            barrier, inc=1, device_id={"pipe": other, "ctx": me}, device_id_type=MESH
        )

    @pl.when(has_right)
    def _():
        pl.semaphore_signal(barrier, inc=1, device_id=at_ctx(me + 2), device_id_type=MESH)

    @pl.when(has_left)
    def _():
        pl.semaphore_signal(barrier, inc=1, device_id=at_ctx(me - 2), device_id_type=MESH)

    for head in range(key_heads):
        own_copy(head, 0).wait()
        own_copy(head, 1).wait()
    pl.semaphore_wait(
        barrier, 3 + has_right.astype(jnp.int32) + has_left.astype(jnp.int32)
    )

    def piece(head, origin, way):
        target = (me + 2, me - 2, sibling)[way]
        return pltpu.make_async_remote_copy(
            src_ref=kv_all.at[head, origin],
            dst_ref=kv_all.at[head, origin],
            send_sem=send_sem.at[way, head, origin],
            recv_sem=recv_sem.at[head, origin],
            device_id=at_ctx(target),
            device_id_type=MESH,
        )

    def send_own(head):
        @pl.when(has_right)
        def _():
            piece(head, me, 0).start()

        @pl.when(has_left)
        def _():
            piece(head, me, 1).start()

        piece(head, me, 2).start()

    def hop(head, step):
        @pl.when(place >= step)
        def _():
            origin = me - 2 * step
            piece(head, origin, 2).wait_recv()

            @pl.when(has_right)
            def _():
                piece(head, origin, 0).start()

            piece(head, origin, 2).start()

        @pl.when(place + step < chips)
        def _():
            origin = me + 2 * step
            piece(head, origin, 2).wait_recv()

            @pl.when(has_left)
            def _():
                piece(head, origin, 1).start()

            piece(head, origin, 2).start()

    def hops(head, low, high):
        lax.fori_loop(low, high, lambda step, c: (hop(head, step), c)[1], 0)

    for head in range(min(LEAD, key_heads)):
        send_own(head)

    row_in = lax.broadcasted_iota(jnp.int32, (rows, rows), 0)
    col_in = lax.broadcasted_iota(jnp.int32, (rows, rows), 1)

    def positions(owner, iota):
        first = layout_ref[0, 0, 2 * owner]
        second = layout_ref[0, 0, 2 * owner + 1]
        return jnp.where(iota < block, first * block + iota, (second - 1) * block + iota)

    query_pos = positions(me, row_in)
    for owner in range(n):
        key_pos = positions(owner, col_in)
        bias[:, owner * rows:(owner + 1) * rows] = jnp.where(key_pos <= query_pos, 0.0, -1e30)

    q_copy.wait()
    hops(0, 1, chips)

    def out_copy(index):
        columns = pl.ds(pl.multiple_of(index * HEAD_SIZE, HEAD_SIZE), HEAD_SIZE)
        return pltpu.make_async_remote_copy(
            src_ref=att.at[:, columns],
            dst_ref=out_ref.at[:, columns],
            send_sem=out_send.at[index],
            recv_sem=out_recv.at[index],
            device_id={"pipe": after, "ctx": me},
            device_id_type=MESH,
        )

    scale = 1.0 / math.sqrt(HEAD_SIZE)
    groups = per_kv // STACK

    for head in range(key_heads):
        if head + LEAD < key_heads:
            send_own(head + LEAD)

        def sibling_wait(chip, c, head=head):
            piece(head, 2 * chip + 1 - core, 2).wait_recv()
            return c

        lax.fori_loop(0, chips, sibling_wait, 0)

        def group(g, c, head=head):
            first = head * per_kv + g * STACK
            keys = kv_all[head, :, :, :HEAD_SIZE].reshape(n * rows, HEAD_SIZE)
            values = kv_all[head, :, :, HEAD_SIZE:].reshape(n * rows, HEAD_SIZE)
            base = pl.multiple_of(first * HEAD_SIZE, HEAD_SIZE)
            q_rows = jnp.concatenate(
                [q_buf[:, pl.ds(base + i * HEAD_SIZE, HEAD_SIZE)] for i in range(STACK)], axis=0
            )
            scores = lax.dot_general(
                q_rows, keys, (((1,), (1,)), ((), ())), preferred_element_type=jnp.float32
            )
            scores = scores.reshape(STACK, rows, n * rows) * scale + bias[...][None]
            row_max = jnp.max(scores, axis=2, keepdims=True)
            expo = jnp.exp(scores - row_max)
            total = jnp.sum(expo, axis=2, keepdims=True)
            weights = expo.astype(jnp.bfloat16).reshape(STACK * rows, n * rows)
            product = jnp.dot(weights, values, preferred_element_type=jnp.float32)
            result = (product.reshape(STACK, rows, HEAD_SIZE) / total).astype(jnp.bfloat16)
            for i in range(STACK):
                att[:, pl.ds(base + i * HEAD_SIZE, HEAD_SIZE)] = result[i]
            for i in range(STACK):
                out_copy(first + i).start()
            if head + 1 < key_heads:
                hops(
                    head + 1,
                    1 + g * (chips - 1) // groups,
                    1 + (g + 1) * (chips - 1) // groups,
                )
            return c

        lax.fori_loop(0, groups, group, 0)

    def finish_piece(head, origin, right, left):
        @pl.when(jnp.logical_and(right, has_right))
        def _():
            piece(head, origin, 0).wait_send()

        @pl.when(jnp.logical_and(left, has_left))
        def _():
            piece(head, origin, 1).wait_send()

        piece(head, origin, 2).wait_send()

    for head in range(key_heads):
        def finish(chip, c, head=head):
            finish_piece(head, 2 * chip + core, chip <= place, chip >= place)
            return c

        lax.fori_loop(0, chips, finish, 0)

    def finish_out(index, c):
        out_copy(index).wait()
        return c

    lax.fori_loop(0, key_heads * per_kv, finish_out, 0)


def on_device(queries, projected_key_value, layout):
    rows, width = queries.shape[2:]
    kv_width = projected_key_value.shape[3]
    key_heads = kv_width // (2 * HEAD_SIZE)
    per_kv = width // (key_heads * HEAD_SIZE)
    heads = key_heads * per_kv
    n = lax.axis_size("ctx")
    sections = lax.axis_size("pipe")
    out = pl.pallas_call(
        functools.partial(kernel, n, sections, key_heads, per_kv),
        out_shape=jax.ShapeDtypeStruct((rows, width), jnp.bfloat16),
        in_specs=[
            pl.BlockSpec(memory_space=pltpu.SMEM),
            pl.BlockSpec(memory_space=pl.ANY),
            pl.BlockSpec(memory_space=pl.ANY),
        ],
        out_specs=pl.BlockSpec(memory_space=pl.ANY),
        scratch_shapes=[
            pltpu.VMEM((rows, width), jnp.bfloat16),
            pltpu.VMEM((key_heads, n, rows, 2 * HEAD_SIZE), jnp.bfloat16),
            pltpu.VMEM((rows, width), jnp.bfloat16),
            pltpu.VMEM((rows, n * rows), jnp.float32),
            pltpu.SemaphoreType.DMA((2 * key_heads + 1,)),
            pltpu.SemaphoreType.DMA((3, key_heads, n)),
            pltpu.SemaphoreType.DMA((key_heads, n)),
            pltpu.SemaphoreType.DMA((heads,)),
            pltpu.SemaphoreType.DMA((heads,)),
        ],
        compiler_params=pltpu.CompilerParams(
            collective_id=0, has_side_effects=True, vmem_limit_bytes=60 * 1024 * 1024
        ),
        name="gather_attend_relay",
    )(layout, queries.reshape(rows, width), projected_key_value.reshape(rows, kv_width))
    return out.reshape(queries.shape)


def solution(mesh):
    placed = (P("pipe", None, "ctx", None), P("pipe", None, "ctx", None), P())
    return jax.shard_map(
        on_device,
        mesh=mesh,
        in_specs=placed,
        out_specs=P("pipe", None, "ctx", None),
        check_vma=False,
    )
```

```python
import functools
import math

import jax
import jax.numpy as jnp
from jax import lax
from jax.experimental import pallas as pl
from jax.experimental.pallas import tpu as pltpu
from jax.sharding import PartitionSpec as P

HEAD_SIZE = 128
MESH = pl.DeviceIdType.MESH
STACK = 2
LEAD = 2
SHIP = 2


def kernel(
    n, sections, key_heads, per_kv,
    layout_ref, q_hbm, kv_hbm, out_ref,
    q_buf, kv_all, att, bias, local_sem, send_sem, recv_sem, out_send, out_recv, ship_send, ship_recv,
):
    rows = q_buf.shape[0]
    block = rows // 2
    chips = n // 2
    section = lax.axis_index("pipe")
    me = lax.axis_index("ctx")
    place = me // 2
    core = me % 2
    width = key_heads * HEAD_SIZE
    stay = key_heads - min(SHIP, key_heads - 1)
    head_width = per_kv * HEAD_SIZE

    def at_ctx(index):
        return {"pipe": section, "ctx": index}

    after = (section + 1) % sections
    before = (section + sections - 1) % sections
    has_right = place < chips - 1
    has_left = place > 0
    sibling = 2 * place + 1 - core

    def own_copy(head, half):
        return pltpu.make_async_copy(
            kv_hbm.at[:, pl.ds(half * width + head * HEAD_SIZE, HEAD_SIZE)],
            kv_all.at[head, me, :, pl.ds(half * HEAD_SIZE, HEAD_SIZE)],
            local_sem.at[2 * head + half],
        )

    def ship_copy(head, what):
        if what == 2:
            columns = pl.ds(head * head_width, head_width)
            source, target = q_hbm.at[:, columns], q_buf.at[:, columns]
        else:
            source = kv_hbm.at[:, pl.ds(what * width + head * HEAD_SIZE, HEAD_SIZE)]
            target = kv_all.at[head, me, :, pl.ds(what * HEAD_SIZE, HEAD_SIZE)]
        return pltpu.make_async_remote_copy(
            src_ref=source,
            dst_ref=target,
            send_sem=ship_send.at[head, what],
            recv_sem=ship_recv.at[head, what],
            device_id={"pipe": after, "ctx": me},
            device_id_type=MESH,
        )

    q_columns = pl.ds(0, stay * head_width)
    q_copy = pltpu.make_async_copy(
        q_hbm.at[:, q_columns], q_buf.at[:, q_columns], local_sem.at[2 * key_heads]
    )
    for head in range(stay):
        own_copy(head, 0).start()
        own_copy(head, 1).start()
    q_copy.start()

    barrier = pltpu.get_barrier_semaphore()
    pl.semaphore_signal(barrier, inc=1, device_id=at_ctx(sibling), device_id_type=MESH)
    for other in (after, before):
        pl.semaphore_signal(
            barrier, inc=1, device_id={"pipe": other, "ctx": me}, device_id_type=MESH
        )

    @pl.when(has_right)
    def _():
        pl.semaphore_signal(barrier, inc=1, device_id=at_ctx(me + 2), device_id_type=MESH)

    @pl.when(has_left)
    def _():
        pl.semaphore_signal(barrier, inc=1, device_id=at_ctx(me - 2), device_id_type=MESH)

    for head in range(stay):
        own_copy(head, 0).wait()
        own_copy(head, 1).wait()
    pl.semaphore_wait(
        barrier, 3 + has_right.astype(jnp.int32) + has_left.astype(jnp.int32)
    )
    for head in range(stay, key_heads):
        ship_copy(head, 0).start()
        ship_copy(head, 1).start()

    def piece(head, origin, way):
        target = (me + 2, me - 2, sibling)[way]
        return pltpu.make_async_remote_copy(
            src_ref=kv_all.at[head, origin],
            dst_ref=kv_all.at[head, origin],
            send_sem=send_sem.at[way, head, origin],
            recv_sem=recv_sem.at[head, origin],
            device_id=at_ctx(target),
            device_id_type=MESH,
        )

    def send_own(head):
        if head >= stay:
            ship_copy(head, 0).wait_recv()
            ship_copy(head, 1).wait_recv()

        @pl.when(has_right)
        def _():
            piece(head, me, 0).start()

        @pl.when(has_left)
        def _():
            piece(head, me, 1).start()

        piece(head, me, 2).start()

    def hop(head, step):
        @pl.when(place >= step)
        def _():
            origin = me - 2 * step
            piece(head, origin, 2).wait_recv()

            @pl.when(has_right)
            def _():
                piece(head, origin, 0).start()

            piece(head, origin, 2).start()

        @pl.when(place + step < chips)
        def _():
            origin = me + 2 * step
            piece(head, origin, 2).wait_recv()

            @pl.when(has_left)
            def _():
                piece(head, origin, 1).start()

            piece(head, origin, 2).start()

    def steps_of(wave):
        return max(1, wave - key_heads + 1), min(wave, chips - 1) + 1

    def hops(wave, low, high):
        lax.fori_loop(low, high, lambda step, c: (hop(wave - step, step), c)[1], 0)

    def own_of(wave):
        if wave == 0:
            for head in range(min(LEAD, key_heads)):
                send_own(head)
        elif wave + LEAD - 1 < key_heads:
            send_own(wave + LEAD - 1)

    own_of(0)
    for head in range(stay, key_heads):
        ship_copy(head, 2).start()

    row_in = lax.broadcasted_iota(jnp.int32, (rows, rows), 0)
    col_in = lax.broadcasted_iota(jnp.int32, (rows, rows), 1)

    def positions(owner, iota):
        first = layout_ref[0, 0, 2 * owner]
        second = layout_ref[0, 0, 2 * owner + 1]
        return jnp.where(iota < block, first * block + iota, (second - 1) * block + iota)

    query_pos = positions(me, row_in)
    for owner in range(n):
        key_pos = positions(owner, col_in)
        bias[:, owner * rows:(owner + 1) * rows] = jnp.where(key_pos <= query_pos, 0.0, -1e30)

    q_copy.wait()
    for wave in range(1, chips):
        own_of(wave)
        hops(wave, *steps_of(wave))

    def out_copy(index):
        columns = pl.ds(pl.multiple_of(index * HEAD_SIZE, HEAD_SIZE), HEAD_SIZE)
        return pltpu.make_async_remote_copy(
            src_ref=att.at[:, columns],
            dst_ref=out_ref.at[:, columns],
            send_sem=out_send.at[index],
            recv_sem=out_recv.at[index],
            device_id={"pipe": after, "ctx": me},
            device_id_type=MESH,
        )

    scale = 1.0 / math.sqrt(HEAD_SIZE)
    groups = per_kv // STACK

    def home_copy(index):
        columns = pl.ds(pl.multiple_of(index * HEAD_SIZE, HEAD_SIZE), HEAD_SIZE)
        return pltpu.make_async_copy(
            att.at[:, columns], out_ref.at[:, columns], out_send.at[index]
        )

    for head in range(key_heads):
        wave = head + chips
        own_of(wave)
        low, high = steps_of(wave)
        if head >= stay:
            ship_copy(head, 2).wait_recv()

        def sibling_wait(chip, c, head=head):
            piece(head, 2 * chip + 1 - core, 2).wait_recv()
            return c

        lax.fori_loop(0, chips, sibling_wait, 0)

        def group(g, c, head=head, wave=wave, low=low, high=high):
            first = head * per_kv + g * STACK
            keys = kv_all[head, :, :, :HEAD_SIZE].reshape(n * rows, HEAD_SIZE)
            values = kv_all[head, :, :, HEAD_SIZE:].reshape(n * rows, HEAD_SIZE)
            base = pl.multiple_of(first * HEAD_SIZE, HEAD_SIZE)
            q_rows = jnp.concatenate(
                [q_buf[:, pl.ds(base + i * HEAD_SIZE, HEAD_SIZE)] for i in range(STACK)], axis=0
            )
            scores = lax.dot_general(
                q_rows, keys, (((1,), (1,)), ((), ())), preferred_element_type=jnp.float32
            )
            scores = scores.reshape(STACK, rows, n * rows) * scale + bias[...][None]
            row_max = jnp.max(scores, axis=2, keepdims=True)
            expo = jnp.exp(scores - row_max)
            total = jnp.sum(expo, axis=2, keepdims=True)
            weights = expo.astype(jnp.bfloat16).reshape(STACK * rows, n * rows)
            product = jnp.dot(weights, values, preferred_element_type=jnp.float32)
            result = (product.reshape(STACK, rows, HEAD_SIZE) / total).astype(jnp.bfloat16)
            for i in range(STACK):
                att[:, pl.ds(base + i * HEAD_SIZE, HEAD_SIZE)] = result[i]
            for i in range(STACK):
                (out_copy if head < stay else home_copy)(first + i).start()
            if high > low:
                hops(
                    wave,
                    low + g * (high - low) // groups,
                    low + (g + 1) * (high - low) // groups,
                )
            return c

        lax.fori_loop(0, groups, group, 0)

    def finish_piece(head, origin, right, left):
        @pl.when(jnp.logical_and(right, has_right))
        def _():
            piece(head, origin, 0).wait_send()

        @pl.when(jnp.logical_and(left, has_left))
        def _():
            piece(head, origin, 1).wait_send()

        piece(head, origin, 2).wait_send()

    for head in range(key_heads):
        def finish(chip, c, head=head):
            finish_piece(head, 2 * chip + core, chip <= place, chip >= place)
            return c

        lax.fori_loop(0, chips, finish, 0)

    def finish_out(index, c):
        out_copy(index).wait()
        return c

    def finish_home(index, c):
        home_copy(index).wait()
        return c

    lax.fori_loop(stay * per_kv, key_heads * per_kv, finish_home, 0)
    for head in range(stay, key_heads):
        for what in range(3):
            ship_copy(head, what).wait_send()
    lax.fori_loop(0, stay * per_kv, finish_out, 0)


def on_device(queries, projected_key_value, layout):
    rows, width = queries.shape[2:]
    kv_width = projected_key_value.shape[3]
    key_heads = kv_width // (2 * HEAD_SIZE)
    per_kv = width // (key_heads * HEAD_SIZE)
    heads = key_heads * per_kv
    n = lax.axis_size("ctx")
    sections = lax.axis_size("pipe")
    out = pl.pallas_call(
        functools.partial(kernel, n, sections, key_heads, per_kv),
        out_shape=jax.ShapeDtypeStruct((rows, width), jnp.bfloat16),
        in_specs=[
            pl.BlockSpec(memory_space=pltpu.SMEM),
            pl.BlockSpec(memory_space=pl.ANY),
            pl.BlockSpec(memory_space=pl.ANY),
        ],
        out_specs=pl.BlockSpec(memory_space=pl.ANY),
        scratch_shapes=[
            pltpu.VMEM((rows, width), jnp.bfloat16),
            pltpu.VMEM((key_heads, n, rows, 2 * HEAD_SIZE), jnp.bfloat16),
            pltpu.VMEM((rows, width), jnp.bfloat16),
            pltpu.VMEM((rows, n * rows), jnp.float32),
            pltpu.SemaphoreType.DMA((2 * key_heads + 1,)),
            pltpu.SemaphoreType.DMA((3, key_heads, n)),
            pltpu.SemaphoreType.DMA((key_heads, n)),
            pltpu.SemaphoreType.DMA((heads,)),
            pltpu.SemaphoreType.DMA((heads,)),
            pltpu.SemaphoreType.DMA((key_heads, 3)),
            pltpu.SemaphoreType.DMA((key_heads, 3)),
        ],
        compiler_params=pltpu.CompilerParams(
            collective_id=0, has_side_effects=True, vmem_limit_bytes=60 * 1024 * 1024
        ),
        name="gather_attend_relay",
    )(layout, queries.reshape(rows, width), projected_key_value.reshape(rows, kv_width))
    return out.reshape(queries.shape)


def solution(mesh):
    placed = (P("pipe", None, "ctx", None), P("pipe", None, "ctx", None), P())
    return jax.shard_map(
        on_device,
        mesh=mesh,
        in_specs=placed,
        out_specs=P("pipe", None, "ctx", None),
        check_vma=False,
    )
```

```python
import functools
import math

import jax
import jax.numpy as jnp
from jax import lax
from jax.experimental import pallas as pl
from jax.experimental.pallas import tpu as pltpu
from jax.sharding import PartitionSpec as P

HEAD_SIZE = 128
MESH = pl.DeviceIdType.MESH
STACK = 2
LEAD = 2
SHIP = 2
SHIP_LEAD = 2
LAST_STACK = 6


def kernel(
    n, sections, key_heads, per_kv,
    layout_ref, q_hbm, kv_hbm, out_ref,
    q_buf, kv_all, att, bias, local_sem, send_sem, recv_sem, out_send, out_recv, ship_send, ship_recv,
):
    rows = q_buf.shape[0]
    block = rows // 2
    chips = n // 2
    section = lax.axis_index("pipe")
    me = lax.axis_index("ctx")
    place = me // 2
    core = me % 2
    width = key_heads * HEAD_SIZE
    stay = key_heads - min(SHIP, key_heads - 1)
    head_width = per_kv * HEAD_SIZE

    def at_ctx(index):
        return {"pipe": section, "ctx": index}

    after = (section + 1) % sections
    before = (section + sections - 1) % sections
    has_right = place < chips - 1
    has_left = place > 0
    sibling = 2 * place + 1 - core

    def own_copy(head, half):
        return pltpu.make_async_copy(
            kv_hbm.at[:, pl.ds(half * width + head * HEAD_SIZE, HEAD_SIZE)],
            kv_all.at[head, me, :, pl.ds(half * HEAD_SIZE, HEAD_SIZE)],
            local_sem.at[2 * head + half],
        )

    def ship_copy(head, what):
        if what == 2:
            columns = pl.ds(head * head_width, head_width)
            source, target = q_hbm.at[:, columns], q_buf.at[:, columns]
        else:
            source = kv_hbm.at[:, pl.ds(what * width + head * HEAD_SIZE, HEAD_SIZE)]
            target = kv_all.at[head, me, :, pl.ds(what * HEAD_SIZE, HEAD_SIZE)]
        return pltpu.make_async_remote_copy(
            src_ref=source,
            dst_ref=target,
            send_sem=ship_send.at[head, what],
            recv_sem=ship_recv.at[head, what],
            device_id={"pipe": after, "ctx": me},
            device_id_type=MESH,
        )

    q_columns = pl.ds(0, stay * head_width)
    q_copy = pltpu.make_async_copy(
        q_hbm.at[:, q_columns], q_buf.at[:, q_columns], local_sem.at[2 * key_heads]
    )
    for head in range(stay):
        own_copy(head, 0).start()
        own_copy(head, 1).start()
    q_copy.start()

    barrier = pltpu.get_barrier_semaphore()
    pl.semaphore_signal(barrier, inc=1, device_id=at_ctx(sibling), device_id_type=MESH)
    for other in (after, before):
        pl.semaphore_signal(
            barrier, inc=1, device_id={"pipe": other, "ctx": me}, device_id_type=MESH
        )

    @pl.when(has_right)
    def _():
        pl.semaphore_signal(barrier, inc=1, device_id=at_ctx(me + 2), device_id_type=MESH)

    @pl.when(has_left)
    def _():
        pl.semaphore_signal(barrier, inc=1, device_id=at_ctx(me - 2), device_id_type=MESH)

    for head in range(stay):
        own_copy(head, 0).wait()
        own_copy(head, 1).wait()
    pl.semaphore_wait(
        barrier, 3 + has_right.astype(jnp.int32) + has_left.astype(jnp.int32)
    )
    for head in range(stay, key_heads):
        ship_copy(head, 0).start()
        ship_copy(head, 1).start()

    def piece(head, origin, way):
        target = (me + 2, me - 2, sibling)[way]
        return pltpu.make_async_remote_copy(
            src_ref=kv_all.at[head, origin],
            dst_ref=kv_all.at[head, origin],
            send_sem=send_sem.at[way, head, origin],
            recv_sem=recv_sem.at[head, origin],
            device_id=at_ctx(target),
            device_id_type=MESH,
        )

    def send_own(head):
        if head >= stay:
            ship_copy(head, 0).wait_recv()
            ship_copy(head, 1).wait_recv()

        @pl.when(has_right)
        def _():
            piece(head, me, 0).start()

        @pl.when(has_left)
        def _():
            piece(head, me, 1).start()

        piece(head, me, 2).start()

    def hop(head, step):
        @pl.when(place >= step)
        def _():
            origin = me - 2 * step
            piece(head, origin, 2).wait_recv()

            @pl.when(has_right)
            def _():
                piece(head, origin, 0).start()

            piece(head, origin, 2).start()

        @pl.when(place + step < chips)
        def _():
            origin = me + 2 * step
            piece(head, origin, 2).wait_recv()

            @pl.when(has_left)
            def _():
                piece(head, origin, 1).start()

            piece(head, origin, 2).start()

    def steps_of(wave):
        return max(1, wave - key_heads + 1), min(wave, chips - 1) + 1

    def hops(wave, low, high):
        lax.fori_loop(low, high, lambda step, c: (hop(wave - step, step), c)[1], 0)

    def own_of(wave):
        if wave == 0:
            for head in range(min(LEAD, stay)):
                send_own(head)
            return
        if LEAD <= wave + LEAD - 1 < stay:
            send_own(wave + LEAD - 1)
        for head in range(stay, key_heads):
            if max(head + 1 - SHIP_LEAD, 1) == wave:
                send_own(head)

    own_of(0)
    for head in range(stay, key_heads):
        ship_copy(head, 2).start()

    row_in = lax.broadcasted_iota(jnp.int32, (rows, rows), 0)
    col_in = lax.broadcasted_iota(jnp.int32, (rows, rows), 1)

    def positions(owner, iota):
        first = layout_ref[0, 0, 2 * owner]
        second = layout_ref[0, 0, 2 * owner + 1]
        return jnp.where(iota < block, first * block + iota, (second - 1) * block + iota)

    query_pos = positions(me, row_in)
    for owner in range(n):
        key_pos = positions(owner, col_in)
        bias[:, owner * rows:(owner + 1) * rows] = jnp.where(key_pos <= query_pos, 0.0, -1e30)

    q_copy.wait()
    for wave in range(1, chips):
        hops(wave, *steps_of(wave))
        own_of(wave)

    def out_copy(index):
        columns = pl.ds(pl.multiple_of(index * HEAD_SIZE, HEAD_SIZE), HEAD_SIZE)
        return pltpu.make_async_remote_copy(
            src_ref=att.at[:, columns],
            dst_ref=out_ref.at[:, columns],
            send_sem=out_send.at[index],
            recv_sem=out_recv.at[index],
            device_id={"pipe": after, "ctx": me},
            device_id_type=MESH,
        )

    scale = 1.0 / math.sqrt(HEAD_SIZE)

    def home_copy(index):
        columns = pl.ds(pl.multiple_of(index * HEAD_SIZE, HEAD_SIZE), HEAD_SIZE)
        return pltpu.make_async_copy(
            att.at[:, columns], out_ref.at[:, columns], out_send.at[index]
        )

    for head in range(key_heads):
        wave = head + chips
        stack = LAST_STACK if head == key_heads - 1 else STACK
        groups = per_kv // stack
        own_of(wave)
        low, high = steps_of(wave)
        if head >= stay:
            ship_copy(head, 2).wait_recv()

        def sibling_wait(chip, c, head=head):
            piece(head, 2 * chip + 1 - core, 2).wait_recv()
            return c

        lax.fori_loop(0, chips, sibling_wait, 0)

        def group(g, c, head=head, wave=wave, low=low, high=high, stack=stack, groups=groups):
            first = head * per_kv + g * stack
            keys = kv_all[head, :, :, :HEAD_SIZE].reshape(n * rows, HEAD_SIZE)
            values = kv_all[head, :, :, HEAD_SIZE:].reshape(n * rows, HEAD_SIZE)
            base = pl.multiple_of(first * HEAD_SIZE, HEAD_SIZE)
            q_rows = jnp.concatenate(
                [q_buf[:, pl.ds(base + i * HEAD_SIZE, HEAD_SIZE)] for i in range(stack)], axis=0
            )
            scores = lax.dot_general(
                q_rows, keys, (((1,), (1,)), ((), ())), preferred_element_type=jnp.float32
            )
            scores = scores.reshape(stack, rows, n * rows) * scale + bias[...][None]
            row_max = jnp.max(scores, axis=2, keepdims=True)
            expo = jnp.exp(scores - row_max)
            total = jnp.sum(expo, axis=2, keepdims=True)
            weights = expo.astype(jnp.bfloat16).reshape(stack * rows, n * rows)
            product = jnp.dot(weights, values, preferred_element_type=jnp.float32)
            result = (product.reshape(stack, rows, HEAD_SIZE) / total).astype(jnp.bfloat16)
            for i in range(stack):
                att[:, pl.ds(base + i * HEAD_SIZE, HEAD_SIZE)] = result[i]
            for i in range(stack):
                (out_copy if head < stay else home_copy)(first + i).start()
            if high > low:
                hops(
                    wave,
                    low + g * (high - low) // groups,
                    low + (g + 1) * (high - low) // groups,
                )
            return c

        lax.fori_loop(0, groups, group, 0)

    def finish_piece(head, origin, right, left):
        @pl.when(jnp.logical_and(right, has_right))
        def _():
            piece(head, origin, 0).wait_send()

        @pl.when(jnp.logical_and(left, has_left))
        def _():
            piece(head, origin, 1).wait_send()

        piece(head, origin, 2).wait_send()

    for head in range(key_heads):
        def finish(chip, c, head=head):
            finish_piece(head, 2 * chip + core, chip <= place, chip >= place)
            return c

        lax.fori_loop(0, chips, finish, 0)

    def finish_out(index, c):
        out_copy(index).wait()
        return c

    def finish_home(index, c):
        home_copy(index).wait()
        return c

    lax.fori_loop(stay * per_kv, key_heads * per_kv, finish_home, 0)
    for head in range(stay, key_heads):
        for what in range(3):
            ship_copy(head, what).wait_send()
    lax.fori_loop(0, stay * per_kv, finish_out, 0)


def write(parts, source, target, sem):
    share = source.shape[0] // parts
    copies = [
        pltpu.make_async_copy(
            source.at[pl.ds(i * share, share)], target.at[pl.ds(i * share, share)], sem.at[i]
        )
        for i in range(parts)
    ]
    for copy in copies:
        copy.start()
    for copy in copies:
        copy.wait()


def vmem_bytes(n, rows, width, kv_width):
    keys = n * rows
    gathered = 2 * keys * kv_width
    scores = 4 * rows * keys
    return gathered + 3 * 2 * rows * width + (3 * max(STACK, LAST_STACK) + 2) * scores + 2 * 1024 * 1024


def on_device(queries, projected_key_value, layout):
    rows, width = queries.shape[2:]
    kv_width = projected_key_value.shape[3]
    key_heads = kv_width // (2 * HEAD_SIZE)
    per_kv = width // (key_heads * HEAD_SIZE)
    heads = key_heads * per_kv
    n = lax.axis_size("ctx")
    sections = lax.axis_size("pipe")
    arrived = pl.pallas_call(
        functools.partial(kernel, n, sections, key_heads, per_kv),
        out_shape=jax.ShapeDtypeStruct((rows, width), jnp.bfloat16),
        in_specs=[
            pl.BlockSpec(memory_space=pltpu.SMEM),
            pl.BlockSpec(memory_space=pltpu.HBM),
            pl.BlockSpec(memory_space=pltpu.HBM),
        ],
        out_specs=pl.BlockSpec(memory_space=pltpu.VMEM),
        scratch_shapes=[
            pltpu.VMEM((rows, width), jnp.bfloat16),
            pltpu.VMEM((key_heads, n, rows, 2 * HEAD_SIZE), jnp.bfloat16),
            pltpu.VMEM((rows, width), jnp.bfloat16),
            pltpu.VMEM((rows, n * rows), jnp.float32),
            pltpu.SemaphoreType.DMA((2 * key_heads + 1,)),
            pltpu.SemaphoreType.DMA((3, key_heads, n)),
            pltpu.SemaphoreType.DMA((key_heads, n)),
            pltpu.SemaphoreType.DMA((heads,)),
            pltpu.SemaphoreType.DMA((heads,)),
            pltpu.SemaphoreType.DMA((key_heads, 3)),
            pltpu.SemaphoreType.DMA((key_heads, 3)),
        ],
        compiler_params=pltpu.CompilerParams(
            collective_id=0, has_side_effects=True, vmem_limit_bytes=vmem_bytes(n, rows, width, kv_width)
        ),
        name="gather_attend_relay",
    )(
        pltpu.with_memory_space_constraint(layout, pltpu.HBM),
        pltpu.with_memory_space_constraint(queries.reshape(rows, width), pltpu.HBM),
        pltpu.with_memory_space_constraint(
            projected_key_value.reshape(rows, kv_width), pltpu.HBM
        ),
    )
    parts = 8
    out = pl.pallas_call(
        functools.partial(write, parts),
        out_shape=jax.ShapeDtypeStruct((rows, width), jnp.bfloat16),
        in_specs=[pl.BlockSpec(memory_space=pltpu.VMEM)],
        out_specs=pl.BlockSpec(memory_space=pltpu.HBM),
        scratch_shapes=[pltpu.SemaphoreType.DMA((parts,))],
        compiler_params=pltpu.CompilerParams(vmem_limit_bytes=8 * 1024 * 1024),
        name="write_back",
    )(arrived)
    return out.reshape(queries.shape)


def solution(mesh):
    placed = (P("pipe", None, "ctx", None), P("pipe", None, "ctx", None), P())
    return jax.shard_map(
        on_device,
        mesh=mesh,
        in_specs=placed,
        out_specs=P("pipe", None, "ctx", None),
        check_vma=False,
    )
```

```python
import functools
import math

import jax
import jax.numpy as jnp
from jax import lax
from jax.experimental import pallas as pl
from jax.experimental.pallas import tpu as pltpu
from jax.sharding import PartitionSpec as P

HEAD_SIZE = 128
MESH = pl.DeviceIdType.MESH
STACK = 2
LEAD = 2
SHIP = 2
SHIP_LEAD = 2
LAST_STACK = 6


def kernel(
    n, sections, key_heads, per_kv,
    layout_ref, q_hbm, kv_hbm, out_ref,
    q_buf, kv_all, att, bias, local_sem, send_sem, recv_sem, out_send, out_recv, ship_send, ship_recv,
):
    rows = q_buf.shape[0]
    block = rows // 2
    chips = n // 2
    section = lax.axis_index("pipe")
    me = lax.axis_index("ctx")
    place = me // 2
    core = me % 2
    width = key_heads * HEAD_SIZE
    stay = key_heads - min(SHIP, key_heads - 1)
    head_width = per_kv * HEAD_SIZE

    def at_ctx(index):
        return {"pipe": section, "ctx": index}

    after = (section + 1) % sections
    before = (section + sections - 1) % sections
    has_right = place < chips - 1
    has_left = place > 0
    sibling = 2 * place + 1 - core
    far_right = place < chips - 2
    far_left = place > 1

    def own_copy(head, half):
        return pltpu.make_async_copy(
            kv_hbm.at[:, pl.ds(half * width + head * HEAD_SIZE, HEAD_SIZE)],
            kv_all.at[head, me, :, pl.ds(half * HEAD_SIZE, HEAD_SIZE)],
            local_sem.at[2 * head + half],
        )

    def ship_copy(head, what):
        if what == 2:
            columns = pl.ds(head * head_width, head_width)
            source, target = q_hbm.at[:, columns], q_buf.at[:, columns]
        else:
            source = kv_hbm.at[:, pl.ds(what * width + head * HEAD_SIZE, HEAD_SIZE)]
            target = kv_all.at[head, me, :, pl.ds(what * HEAD_SIZE, HEAD_SIZE)]
        return pltpu.make_async_remote_copy(
            src_ref=source,
            dst_ref=target,
            send_sem=ship_send.at[head, what],
            recv_sem=ship_recv.at[head, what],
            device_id={"pipe": after, "ctx": me},
            device_id_type=MESH,
        )

    q_columns = pl.ds(0, stay * head_width)
    q_copy = pltpu.make_async_copy(
        q_hbm.at[:, q_columns], q_buf.at[:, q_columns], local_sem.at[2 * key_heads]
    )
    for head in range(stay):
        own_copy(head, 0).start()
        own_copy(head, 1).start()
    q_copy.start()

    barrier = pltpu.get_barrier_semaphore()
    pl.semaphore_signal(barrier, inc=1, device_id=at_ctx(sibling), device_id_type=MESH)
    for other in (after, before):
        pl.semaphore_signal(
            barrier, inc=1, device_id={"pipe": other, "ctx": me}, device_id_type=MESH
        )

    @pl.when(has_right)
    def _():
        pl.semaphore_signal(barrier, inc=1, device_id=at_ctx(me + 2), device_id_type=MESH)

    @pl.when(has_left)
    def _():
        pl.semaphore_signal(barrier, inc=1, device_id=at_ctx(me - 2), device_id_type=MESH)

    @pl.when(far_right)
    def _():
        pl.semaphore_signal(barrier, inc=1, device_id=at_ctx(me + 4), device_id_type=MESH)

    @pl.when(far_left)
    def _():
        pl.semaphore_signal(barrier, inc=1, device_id=at_ctx(me - 4), device_id_type=MESH)

    for head in range(stay):
        own_copy(head, 0).wait()
        own_copy(head, 1).wait()
    pl.semaphore_wait(
        barrier,
        3 + has_right.astype(jnp.int32) + has_left.astype(jnp.int32)
        + far_right.astype(jnp.int32) + far_left.astype(jnp.int32),
    )
    for head in range(stay, key_heads):
        ship_copy(head, 0).start()
        ship_copy(head, 1).start()

    def piece(head, origin, way):
        target = (me + 2, me - 2, sibling, me + 4, me - 4)[way]
        return pltpu.make_async_remote_copy(
            src_ref=kv_all.at[head, origin],
            dst_ref=kv_all.at[head, origin],
            send_sem=send_sem.at[way, head, origin],
            recv_sem=recv_sem.at[head, origin],
            device_id=at_ctx(target),
            device_id_type=MESH,
        )

    def send_own(head):
        if head >= stay:
            ship_copy(head, 0).wait_recv()
            ship_copy(head, 1).wait_recv()

        @pl.when(has_right)
        def _():
            piece(head, me, 0).start()

        @pl.when(has_left)
        def _():
            piece(head, me, 1).start()

        @pl.when(far_right)
        def _():
            piece(head, me, 3).start()

        @pl.when(far_left)
        def _():
            piece(head, me, 4).start()

        piece(head, me, 2).start()

    def hop(head, step):
        @pl.when(place >= step)
        def _():
            origin = me - 2 * step
            piece(head, origin, 2).wait_recv()

            @pl.when(jnp.logical_and(has_right, step > 1))
            def _():
                piece(head, origin, 0).start()

            piece(head, origin, 2).start()

        @pl.when(place + step < chips)
        def _():
            origin = me + 2 * step
            piece(head, origin, 2).wait_recv()

            @pl.when(jnp.logical_and(has_left, step > 1))
            def _():
                piece(head, origin, 1).start()

            piece(head, origin, 2).start()

    def steps_of(wave):
        return max(1, wave - key_heads + 1), min(wave, chips - 1) + 1

    def hops(wave, low, high):
        lax.fori_loop(low, high, lambda step, c: (hop(wave - step, step), c)[1], 0)

    def own_of(wave):
        if wave == 0:
            for head in range(min(LEAD, stay)):
                send_own(head)
            return
        if LEAD <= wave + LEAD - 1 < stay:
            send_own(wave + LEAD - 1)
        for head in range(stay, key_heads):
            if max(head + 1 - SHIP_LEAD, 1) == wave:
                send_own(head)

    own_of(0)
    for head in range(stay, key_heads):
        ship_copy(head, 2).start()

    row_in = lax.broadcasted_iota(jnp.int32, (rows, rows), 0)
    col_in = lax.broadcasted_iota(jnp.int32, (rows, rows), 1)

    def positions(owner, iota):
        first = layout_ref[0, 0, 2 * owner]
        second = layout_ref[0, 0, 2 * owner + 1]
        return jnp.where(iota < block, first * block + iota, (second - 1) * block + iota)

    query_pos = positions(me, row_in)
    for owner in range(n):
        key_pos = positions(owner, col_in)
        bias[:, owner * rows:(owner + 1) * rows] = jnp.where(key_pos <= query_pos, 0.0, -1e30)

    q_copy.wait()
    for wave in range(1, chips):
        hops(wave, *steps_of(wave))
        own_of(wave)

    def out_copy(index):
        columns = pl.ds(pl.multiple_of(index * HEAD_SIZE, HEAD_SIZE), HEAD_SIZE)
        return pltpu.make_async_remote_copy(
            src_ref=att.at[:, columns],
            dst_ref=out_ref.at[:, columns],
            send_sem=out_send.at[index],
            recv_sem=out_recv.at[index],
            device_id={"pipe": after, "ctx": me},
            device_id_type=MESH,
        )

    scale = 1.0 / math.sqrt(HEAD_SIZE)

    def home_copy(index):
        columns = pl.ds(pl.multiple_of(index * HEAD_SIZE, HEAD_SIZE), HEAD_SIZE)
        return pltpu.make_async_copy(
            att.at[:, columns], out_ref.at[:, columns], out_send.at[index]
        )

    for head in range(key_heads):
        wave = head + chips
        stack = LAST_STACK if head == key_heads - 1 else STACK
        groups = per_kv // stack
        own_of(wave)
        low, high = steps_of(wave)
        if head >= stay:
            ship_copy(head, 2).wait_recv()

        def sibling_wait(chip, c, head=head):
            piece(head, 2 * chip + 1 - core, 2).wait_recv()
            return c

        lax.fori_loop(0, chips, sibling_wait, 0)

        def group(g, c, head=head, wave=wave, low=low, high=high, stack=stack, groups=groups):
            first = head * per_kv + g * stack
            keys = kv_all[head, :, :, :HEAD_SIZE].reshape(n * rows, HEAD_SIZE)
            values = kv_all[head, :, :, HEAD_SIZE:].reshape(n * rows, HEAD_SIZE)
            base = pl.multiple_of(first * HEAD_SIZE, HEAD_SIZE)
            q_rows = jnp.concatenate(
                [q_buf[:, pl.ds(base + i * HEAD_SIZE, HEAD_SIZE)] for i in range(stack)], axis=0
            )
            scores = lax.dot_general(
                q_rows, keys, (((1,), (1,)), ((), ())), preferred_element_type=jnp.float32
            )
            scores = scores.reshape(stack, rows, n * rows) * scale + bias[...][None]
            row_max = jnp.max(scores, axis=2, keepdims=True)
            expo = jnp.exp(scores - row_max)
            total = jnp.sum(expo, axis=2, keepdims=True)
            weights = expo.astype(jnp.bfloat16).reshape(stack * rows, n * rows)
            product = jnp.dot(weights, values, preferred_element_type=jnp.float32)
            result = (product.reshape(stack, rows, HEAD_SIZE) / total).astype(jnp.bfloat16)
            for i in range(stack):
                att[:, pl.ds(base + i * HEAD_SIZE, HEAD_SIZE)] = result[i]
            for i in range(stack):
                (out_copy if head < stay else home_copy)(first + i).start()
            if high > low:
                hops(
                    wave,
                    low + g * (high - low) // groups,
                    low + (g + 1) * (high - low) // groups,
                )
            return c

        lax.fori_loop(0, groups, group, 0)

    def finish_piece(head, origin, right, left):
        @pl.when(jnp.logical_and(right, has_right))
        def _():
            piece(head, origin, 0).wait_send()

        @pl.when(jnp.logical_and(left, has_left))
        def _():
            piece(head, origin, 1).wait_send()

        piece(head, origin, 2).wait_send()

    for head in range(key_heads):
        def finish(chip, c, head=head):
            finish_piece(
                head, 2 * chip + core,
                jnp.logical_and(chip <= place, chip != place - 1),
                jnp.logical_and(chip >= place, chip != place + 1),
            )
            return c

        lax.fori_loop(0, chips, finish, 0)

        @pl.when(far_right)
        def _(head=head):
            piece(head, me, 3).wait_send()

        @pl.when(far_left)
        def _(head=head):
            piece(head, me, 4).wait_send()

    def finish_out(index, c):
        out_copy(index).wait()
        return c

    def finish_home(index, c):
        home_copy(index).wait()
        return c

    lax.fori_loop(stay * per_kv, key_heads * per_kv, finish_home, 0)
    for head in range(stay, key_heads):
        for what in range(3):
            ship_copy(head, what).wait_send()
    lax.fori_loop(0, stay * per_kv, finish_out, 0)


def write(parts, source, target, sem):
    share = source.shape[0] // parts
    copies = [
        pltpu.make_async_copy(
            source.at[pl.ds(i * share, share)], target.at[pl.ds(i * share, share)], sem.at[i]
        )
        for i in range(parts)
    ]
    for copy in copies:
        copy.start()
    for copy in copies:
        copy.wait()


def vmem_bytes(n, rows, width, kv_width):
    keys = n * rows
    gathered = 2 * keys * kv_width
    scores = 4 * rows * keys
    return gathered + 3 * 2 * rows * width + (3 * max(STACK, LAST_STACK) + 2) * scores + 2 * 1024 * 1024


def on_device(queries, projected_key_value, layout):
    rows, width = queries.shape[2:]
    kv_width = projected_key_value.shape[3]
    key_heads = kv_width // (2 * HEAD_SIZE)
    per_kv = width // (key_heads * HEAD_SIZE)
    heads = key_heads * per_kv
    n = lax.axis_size("ctx")
    sections = lax.axis_size("pipe")
    arrived = pl.pallas_call(
        functools.partial(kernel, n, sections, key_heads, per_kv),
        out_shape=jax.ShapeDtypeStruct((rows, width), jnp.bfloat16),
        in_specs=[
            pl.BlockSpec(memory_space=pltpu.SMEM),
            pl.BlockSpec(memory_space=pltpu.HBM),
            pl.BlockSpec(memory_space=pltpu.HBM),
        ],
        out_specs=pl.BlockSpec(memory_space=pltpu.VMEM),
        scratch_shapes=[
            pltpu.VMEM((rows, width), jnp.bfloat16),
            pltpu.VMEM((key_heads, n, rows, 2 * HEAD_SIZE), jnp.bfloat16),
            pltpu.VMEM((rows, width), jnp.bfloat16),
            pltpu.VMEM((rows, n * rows), jnp.float32),
            pltpu.SemaphoreType.DMA((2 * key_heads + 1,)),
            pltpu.SemaphoreType.DMA((5, key_heads, n)),
            pltpu.SemaphoreType.DMA((key_heads, n)),
            pltpu.SemaphoreType.DMA((heads,)),
            pltpu.SemaphoreType.DMA((heads,)),
            pltpu.SemaphoreType.DMA((key_heads, 3)),
            pltpu.SemaphoreType.DMA((key_heads, 3)),
        ],
        compiler_params=pltpu.CompilerParams(
            collective_id=0, has_side_effects=True, vmem_limit_bytes=vmem_bytes(n, rows, width, kv_width)
        ),
        name="gather_attend_relay",
    )(
        pltpu.with_memory_space_constraint(layout, pltpu.HBM),
        pltpu.with_memory_space_constraint(queries.reshape(rows, width), pltpu.HBM),
        pltpu.with_memory_space_constraint(
            projected_key_value.reshape(rows, kv_width), pltpu.HBM
        ),
    )
    parts = 8
    out = pl.pallas_call(
        functools.partial(write, parts),
        out_shape=jax.ShapeDtypeStruct((rows, width), jnp.bfloat16),
        in_specs=[pl.BlockSpec(memory_space=pltpu.VMEM)],
        out_specs=pl.BlockSpec(memory_space=pltpu.HBM),
        scratch_shapes=[pltpu.SemaphoreType.DMA((parts,))],
        compiler_params=pltpu.CompilerParams(vmem_limit_bytes=8 * 1024 * 1024),
        name="write_back",
    )(arrived)
    return out.reshape(queries.shape)


def solution(mesh):
    placed = (P("pipe", None, "ctx", None), P("pipe", None, "ctx", None), P())
    return jax.shard_map(
        on_device,
        mesh=mesh,
        in_specs=placed,
        out_specs=P("pipe", None, "ctx", None),
        check_vma=False,
    )
```
